128 devices in a mesh: grp: 4 (over z), exp: 8 (over x, core), ten: 4 (over y).
Axes of the slice: x: 4, y: 4, z: 4, core: 2. Of those that a mesh axis runs over, the one named last changes fastest.
Arguments:
- tokens: bfloat16 [4096, 4096], P(('grp', 'exp', 'ten')), parts along dimension 0, may hold values from -100 to 100
- norm_gain: float32 [4096], replicated, may hold values from 0.1 to 1.9
- expert_ids: int32 [4096, 8], P(('grp', 'exp', 'ten')), parts along dimension 0, may hold values from 0 to 15, as said below
- gate_prob: float32 [4096, 8], P(('grp', 'exp', 'ten')), parts along dimension 0, may hold values from 0.05 to 1
- w_gate: bfloat16 [16, 4096, 1536], P('exp', None, 'ten'), may hold values from -0.09375 to 0.09375
- w_up: bfloat16 [16, 4096, 1536], P('exp', None, 'ten'), may hold values from -0.09375 to 0.09375
- w_down: bfloat16 [16, 1536, 4096], P('exp', 'ten'), may hold values from -0.15625 to 0.15625
Outputs:
- mixed: bfloat16 [4096, 4096], P(('grp', 'exp', 'ten')), parts along dimension 0
The draws below stay inside these ranges and needn't reach their ends.
There are 4 independent parts, one for each index of `grp`. The reference program is written for one: setup_inputs(seed, part) draws one part's arguments, and reference() takes and returns one part's arrays. A program takes and returns all parts, laid end to end along the dimension named above; an argument that names none is the same for every part. Nothing has to cross between parts.
Inputs may be any that keep to these rules, and one draw needn't show every extreme that they name: `expert_ids`: each row names 8 different experts. Within the rows of one device no expert is named by more than 24 rows, and in every draw one expert is named by exactly 24 rows of every device.
All inputs are finite; a program needn't handle non-finite values.
Results may differ from the reference program's by a relative error of at most 0.012.
Values may be sent and summed in bfloat16 or wider, within the bound.
A program may use at most 128 MiB of HBM per device.

```python
import math
import jax
import jax.numpy as jnp
from jax import lax

D = 4096
FF = 1536
TOP = 8
EXPERTS = 16
TOK_DEV = 32
CAP = 24
TOKENS = 1024
N_TEN = 4


def draw_tokens(key, part):
    key_rows, key_cols, key_base = jax.random.split(key, 3)
    row_scale = jnp.exp(jax.random.uniform(key_rows, (TOKENS, 1)) * math.log(10.0))
    col_scale = jnp.exp(jax.random.uniform(key_cols, (1, D)) * math.log(10.0))
    base_values = jnp.clip(jax.random.normal(key_base, (TOKENS, D)), -4.0, 4.0)
    return (base_values * row_scale * col_scale * 0.25).astype(jnp.bfloat16)


def shuffle_experts(block_key):
    return jax.random.permutation(block_key, EXPERTS)


def shuffle_tokens(block_key):
    return jax.random.permutation(block_key, TOK_DEV)


def pick_experts(order, columns):
    return order[columns]


def draw_expert_ids(key, part):
    blocks = TOKENS // TOK_DEV
    key_hot, key_perm, key_rank, key_start = jax.random.split(jax.random.fold_in(key, 7), 4)
    hot_expert = jax.random.randint(key_hot, (), 0, EXPERTS)
    orders = jax.vmap(shuffle_experts)(jax.random.split(key_perm, blocks))
    places = jnp.arange(EXPERTS, dtype=jnp.int32)[None, :]
    displaced = orders[:, TOP - 1:TOP]
    orders = jnp.where(orders == hot_expert, displaced, jnp.where(places == TOP - 1, hot_expert, orders))
    ranking = jax.vmap(shuffle_tokens)(jax.random.split(key_rank, blocks))
    free_start = jax.random.randint(key_start, (blocks, TOK_DEV), 0, TOP)
    window_start = jnp.where(ranking < TOK_DEV // 4, EXPERTS - 1, jnp.where(ranking < TOK_DEV // 2, TOP - 1, free_start))
    columns = (window_start[:, :, None] + jnp.arange(TOP, dtype=jnp.int32)[None, None, :]) % EXPERTS
    chosen = jax.vmap(pick_experts)(orders, columns)
    return chosen.reshape(TOKENS, TOP).astype(jnp.int32)


def block_levels(rng, dims, pieces, smallest, high):
    def one(axis_at, parts):
        heights = jax.random.uniform(jax.random.fold_in(jax.random.fold_in(rng, 6), axis_at), (parts,), jnp.float32, smallest / len(pieces), high / len(pieces))
        return jnp.repeat(jnp.exp(heights), dims[axis_at] // parts).reshape((-1,) + (1,) * (len(dims) - axis_at - 1))

    gain = one(*pieces[0])
    for cut in pieces[1:]:
        gain = gain * one(*cut)
    return gain


def scatter_about(key, dims, spread, most, pieces=(), kind=jnp.bfloat16):
    entries = jax.random.normal(key, dims, jnp.float32) * spread
    if len(pieces) > 0:
        entries = block_levels(key, dims, pieces, -0.22, 0.18) * entries
    return jnp.clip(entries, min=-most, max=most).astype(kind)


def setup_inputs(seed: int = 0, part: int = 0) -> dict:
    key_list = jax.random.split(jax.random.key(seed), 8)
    part_keys = jax.random.split(jax.random.fold_in(key_list[7], part), 8)
    tokens = draw_tokens(jax.random.fold_in(jax.random.fold_in(key_list[7], part), 71), part)
    norm_gain = jnp.clip(1.0 + 0.18 * jax.random.normal(key_list[1], (D,), jnp.float32), 0.1, 1.9)
    expert_ids = draw_expert_ids(jax.random.fold_in(jax.random.fold_in(key_list[7], part), 71), part)
    gate_prob = jnp.clip(jnp.exp(math.log(1.0) - 2.9957323 * jax.random.uniform(part_keys[3], (TOKENS, TOP), jnp.float32) ** block_levels(part_keys[3], (TOKENS, TOP), ((0, 32),), -0.2, 0.2)), 0.05, 1.0)
    w_gate = scatter_about(key_list[4], (EXPERTS, D, FF), D ** -0.5, 0.09375, ((0, 8), (2, 4)))
    w_up = scatter_about(key_list[5], (EXPERTS, D, FF), D ** -0.5, 0.09375, ((0, 8), (2, 4)))
    w_down = scatter_about(key_list[6], (EXPERTS, FF, D), FF ** -0.5, 0.15625, ((0, 8), (1, 4)))
    return {"tokens": tokens, "norm_gain": norm_gain, "expert_ids": expert_ids, "gate_prob": gate_prob, "w_gate": w_gate, "w_up": w_up, "w_down": w_down}


def expert_rows(rows, weight_gate, weight_up, weight_down):
    gate_part = jnp.dot(rows, weight_gate, preferred_element_type=jnp.float32)
    up_part = jnp.dot(rows, weight_up, preferred_element_type=jnp.float32)
    hidden = (jax.nn.silu(gate_part) * up_part).astype(jnp.bfloat16)
    group_width = FF // N_TEN
    total = jnp.zeros((rows.shape[0], D), jnp.float32)
    for group in range(N_TEN):
        lower = group * group_width
        upper = lower + group_width
        term = jnp.dot(hidden[:, lower:upper], weight_down[lower:upper], preferred_element_type=jnp.float32).astype(jnp.bfloat16)
        total = total + lax.optimization_barrier(term).astype(jnp.float32)
    return total.astype(jnp.bfloat16)

def reference(tokens, norm_gain, expert_ids, gate_prob, w_gate, w_up, w_down):
    floats = tokens.astype(jnp.float32)
    meansq = lax.optimization_barrier(jnp.mean(floats * floats, axis=1, keepdims=True))
    normed = (floats * lax.rsqrt(meansq + 1e-06) * norm_gain).astype(jnp.bfloat16)
    mixing = gate_prob / lax.optimization_barrier(jnp.sum(gate_prob, axis=1, keepdims=True))
    blocks = TOKENS // TOK_DEV
    assigned = TOK_DEV * TOP
    block_ids = expert_ids.reshape(blocks, assigned)
    member = (block_ids[:, :, None] == jnp.arange(EXPERTS, dtype=jnp.int32)[None, None, :]).astype(jnp.int32)
    earlier = jnp.cumsum(member, axis=1) - member
    slot_index = lax.optimization_barrier(jnp.sum(earlier * member, axis=2))
    target = (block_ids * CAP + slot_index).astype(jnp.int32)
    source_rows = normed.reshape(blocks, TOK_DEV, D)
    token_of = (jnp.arange(assigned, dtype=jnp.int32) // TOP).astype(jnp.int32)
    block_of = jnp.arange(blocks, dtype=jnp.int32)[:, None]
    buffer = jnp.zeros((blocks, EXPERTS * CAP, D), jnp.bfloat16)
    buffer = buffer.at[block_of, target].set(source_rows[:, token_of])
    per_expert = buffer.reshape(blocks, EXPERTS, CAP, D).transpose(1, 0, 2, 3).reshape(EXPERTS, blocks * CAP, D)
    outputs = lax.map(lambda item: expert_rows(item[0], item[1], item[2], item[3]), (per_expert, w_gate, w_up, w_down))
    outputs = outputs.reshape(EXPERTS, blocks, CAP, D).transpose(1, 0, 2, 3).reshape(blocks, EXPERTS * CAP, D)
    picked = outputs[block_of, target].reshape(TOKENS, TOP, D)
    mixed = lax.optimization_barrier(jnp.sum(mixing[:, :, None] * picked.astype(jnp.float32), axis=1))
    return mixed.astype(jnp.bfloat16)
```

```python
import jax
import jax.numpy as jnp
from jax import lax
from jax.sharding import PartitionSpec as P


def per_device(tokens, norm_gain, expert_ids, gate_prob, w_gate, w_up, w_down):
    tok_rows, width = tokens.shape
    local_count, _, hid = w_gate.shape
    expert_count = local_count * lax.axis_size("exp")
    floats = tokens.astype(jnp.float32)
    meansq = jnp.mean(floats * floats, axis=1, keepdims=True)
    normed = (floats * lax.rsqrt(meansq + 1e-06) * norm_gain).astype(jnp.bfloat16)
    mixing = gate_prob / jnp.sum(gate_prob, axis=1, keepdims=True)
    chosen = expert_ids[:, :, None] == jnp.arange(expert_count, dtype=jnp.int32)[None, None, :]
    weight = jnp.sum(jnp.where(chosen, mixing[:, :, None], 0.0), axis=1)
    everyone = lax.all_gather(normed, ("exp", "ten"), axis=0, tiled=True)
    weights = lax.all_gather(weight, ("exp", "ten"), axis=0, tiled=True)
    mine = lax.dynamic_slice_in_dim(weights, lax.axis_index("exp") * local_count, local_count, axis=1)
    gate_part = jnp.einsum("td,edf->tef", everyone, w_gate, preferred_element_type=jnp.float32)
    up_part = jnp.einsum("td,edf->tef", everyone, w_up, preferred_element_type=jnp.float32)
    hidden = jax.nn.silu(gate_part) * up_part * mine[:, :, None]
    hidden = hidden.astype(jnp.bfloat16).reshape(-1, local_count * hid)
    partial = jnp.dot(hidden, w_down.reshape(local_count * hid, width), preferred_element_type=jnp.float32)
    return lax.psum_scatter(partial.astype(jnp.bfloat16), ("exp", "ten"), scatter_dimension=0, tiled=True)


def solution(mesh):
    placed = (
        P(("grp", "exp", "ten"), None),
        P(),
        P(("grp", "exp", "ten"), None),
        P(("grp", "exp", "ten"), None),
        P("exp", None, "ten"),
        P("exp", None, "ten"),
        P("exp", "ten", None),
    )
    return jax.shard_map(
        per_device,
        mesh=mesh,
        in_specs=placed,
        out_specs=P(("grp", "exp", "ten"), None),
        check_vma=False,
    )
```

```python
import functools

import jax
import jax.numpy as jnp
from jax import lax
from jax.experimental import pallas as pl
from jax.experimental.pallas import tpu as pltpu
from jax.sharding import PartitionSpec as P

MESH = pl.DeviceIdType.MESH
BF16, F32 = jnp.bfloat16, jnp.float32
SIDE = 4
ROWS = 16
EXTRA = 128
PIECES = 4
DIRS = (1, -1)
ORDER = (0, 1, 3, 2)
RATE, SIB_RATE = 46.5e3, 200e3
LAT, SIB_LAT = 1.7, 1.1
T_UP, T_DOWN, T_ADD = 1.75, 0.55, 0.12


def fw(d):
    return 0 if d == 1 else 1


def toward(h):
    return 1 if h == 0 else -1


def axis_of(s, second):
    return (s + second) % 2


def plan(width):
    block = ROWS * width * 2
    msgs = {}
    tasks = {}

    def msg(key, link, size):
        msgs[key] = (link, size)

    def task(key, needs, after, dur, sends, prio):
        tasks[key] = (needs, after, dur, sends, prio)

    rank = {df: i for i, df in enumerate(ORDER)}
    for s in (0, 1):
        for d in DIRS:
            for h in (0, 1):
                msg(("m1", s, d, h), (axis_of(s, 0), d), block / 2)
                msg(("r4", s, d, h), (axis_of(s, 0), d), block / 2)
            msg(("m2", s, d), (axis_of(s, 0), d), block / 2)
            msg(("r3", s, d), (axis_of(s, 0), d), block / 2)
            for df in range(SIDE):
                for h in (0, 1):
                    msg(("m3", df, s, d, h), (axis_of(s, 1), d), block / 2)
                    msg(("r2", df, s, d, h), (axis_of(s, 1), d), block / 2)
                msg(("m4", df, s, d), (axis_of(s, 1), d), block / 2)
                msg(("r1", df, s, d), (axis_of(s, 1), d), block / 2)
        for df in range(SIDE):
            for dg in range(SIDE):
                msg(("m5", df, s, dg), "sib", block)
    for df in range(SIDE):
        for n in range(PIECES):
            msg(("r0", df, n), "sib", 8 * block / PIECES)

    first = []
    for h in (0, 1):
        for s in (0, 1):
            first += [("m3", 0, s, d, h if d == 1 else 1 - h) for d in DIRS]
    for h in (0, 1):
        for s in (0, 1):
            first += [("m1", s, d, h if d == 1 else 1 - h) for d in DIRS]
    first += [("m5", 0, s, 0) for s in (0, 1)]
    task(("own",), [], [], 0.0, first, (-1,))
    for s in (0, 1):
        for d in DIRS:
            for h in (0, 1):
                df = -d % SIDE
                ahead = [("m2", s, d)] if h == fw(d) else []
                onward = [("m3", df, s, toward(h), h), ("m3", df, s, -toward(h), h)]
                task(("a1", s, d, h), [("m1", s, d, h)], [], 0.0, ahead + onward, (0, rank[df]))
            h = fw(d)
            onward = [("m3", 2, s, toward(h), h), ("m3", 2, s, -toward(h), h)]
            task(("a2", s, d), [("m2", s, d)], [], 0.0, onward, (0, rank[2]))
            for df in range(SIDE):
                task(("a3", df, s, d), [("m3", df, s, d, fw(d))], [], 0.0, [("m4", df, s, d)], (0, rank[df]))
        for df in range(SIDE):
            for dg in range(SIDE):
                if dg == 2:
                    needs = [("m4", df, s, d) for d in DIRS]
                elif dg:
                    needs = [("m3", df, s, 1 if dg == 3 else -1, h) for h in (0, 1)]
                elif df == 2:
                    needs = [("m2", s, d) for d in DIRS]
                elif df:
                    needs = [("m1", s, 1 if df == 3 else -1, h) for h in (0, 1)]
                else:
                    continue
                task(("a5", df, s, dg), needs, [], 0.0, [("m5", df, s, dg)], (1, rank[df]))
    for df in range(SIDE):
        blocks = [("m5", df, s, dg) for s in (0, 1) for dg in range(SIDE)]
        sent = [("a5",) + b[1:] for b in blocks if b[1] or b[3]]
        for l in (0, 1):
            task(("U", df, l), blocks, sent + ([("U", df, 0)] if l else []), T_UP, [], (9, rank[df], 0, l))
        for n in range(PIECES):
            before = [("D", df, n - 1)] if n else [("U", df, 1)]
            task(("D", df, n), [], before, T_DOWN, [("r0", df, n)], (9, rank[df], 1, n))
        for h in (0, 1):
            t = toward(h)
            parts = range(h * PIECES // 2, (h + 1) * PIECES // 2)
            sends = [("r1", df, s, t) for s in (0, 1)] + [("r2", df, s, -t, h) for s in (0, 1)]
            task(("p2", df, h), [("r0", df, n) for n in parts], [], 4 * T_ADD, sends, (3, rank[df]))
            for s in (0, 1):
                after = [("p2", df, h)]
                task(("p13", df, s, h), [("r1", df, s, t)], after, T_ADD, [("r2", df, s, t, h)], (2, rank[df]))
                needs = [("r2", df, s, d, h) for d in DIRS]
                if df == 2:
                    sends = [("r3", s, t)]
                elif df:
                    d = 1 if df == 1 else -1
                    if h == fw(d):
                        needs = needs + [("r3", s, d)]
                    sends = [("r4", s, d, h)]
                else:
                    needs = needs + [("r4", s, d, h) for d in DIRS]
                    sends = []
                task(("p0", df, s, h), needs, after, T_ADD, sends, (2, rank[df]))

    free = {}
    arrive = {}
    done = {}
    order = []
    now = 0.0
    pending = dict(tasks)
    while pending:
        best = None
        for key, (needs, after, dur, sends, prio) in pending.items():
            if any(n not in arrive for n in needs) or any(a not in done for a in after):
                continue
            at = max([now] + [arrive[n] for n in needs])
            rankkey = (at, prio, str(key))
            if best is None or rankkey < best[0]:
                best = (rankkey, key)
        (at, _, _), key = best
        needs, after, dur, sends, prio = pending.pop(key)
        now = at + dur + 0.01
        done[key] = now
        order.append(key)
        for m in sends:
            link, size = msgs[m]
            rate, lat = (SIB_RATE, SIB_LAT) if link == "sib" else (RATE, LAT)
            end = max(free.get(link, 0.0), now) + size / rate
            free[link] = end
            arrive[m] = end + lat
    return order, tasks, list(msgs), now, done, free


def kernel(order, tasks, names, tokens, gain, ids, prob, wg, wu, wd, out,
           xbuf, w1, w2, hid, ybuf, sib, halves, fulls, halves2, fulls2, wsem, ssem, rsem):
    exp, ten = lax.axis_index("exp"), lax.axis_index("ten")
    cx, core = exp // 2, exp % 2
    width = tokens.shape[1]
    half = width // 2
    hidden = wg.shape[2]
    local = wg.shape[0]
    xcut = (width + EXTRA) // 256 * 128 + 128

    def device(axis, d):
        if axis == 0:
            return {"exp": (cx + SIDE + d) % SIDE * 2 + core, "ten": ten}
        return {"exp": exp, "ten": (ten + SIDE + d) % SIDE}

    other = {"exp": cx * 2 + 1 - core, "ten": ten}
    partners = [device(a, d) for a in (0, 1) for d in DIRS] + [other]
    barrier = pltpu.get_barrier_semaphore()
    for p in partners:
        pl.semaphore_signal(barrier, inc=1, device_id=p, device_id_type=MESH)

    loads = []
    for l in range(local):
        loads.append(pltpu.make_async_copy(wg.at[l], w1.at[l, :, pl.ds(0, hidden)], wsem.at[3 * l]))
        loads.append(pltpu.make_async_copy(wu.at[l], w1.at[l, :, pl.ds(hidden, hidden)], wsem.at[3 * l + 1]))
    for l in range(local):
        loads.append(pltpu.make_async_copy(wd.at[l], w2.at[pl.ds(l * hidden, hidden)], wsem.at[3 * l + 2]))
    for c in loads:
        c.start()

    def rows(k, s, dg):
        return pl.ds(((k * 2 + s) * SIDE + dg % SIDE) * ROWS, ROWS)

    def xcols(h):
        return pl.ds(0, xcut) if h == 0 else pl.ds(xcut, width + EXTRA - xcut)

    def ycols(h):
        return pl.ds(h * half, half)

    def xat(df, k, s, dg, h=None):
        if h is None:
            return xbuf.at[df % SIDE, rows(k, s, dg)]
        return xbuf.at[df % SIDE, rows(k, s, dg), xcols(h)]

    def yat(df, k, s, dg, h):
        return ybuf.at[df % SIDE, rows(k, s, dg), ycols(h)]

    def ends(key):
        kind = key[0]
        if kind == "m1":
            _, s, d, h = key
            return xat(0, 0, s, 0, h), xat(-d, 0, s, 0, h), device(axis_of(s, 0), d)
        if kind == "m2":
            _, s, d = key
            return xat(-d, 0, s, 0, fw(d)), xat(2, 0, s, 0, fw(d)), device(axis_of(s, 0), d)
        if kind == "m3":
            _, df, s, d, h = key
            return xat(df, 0, s, 0, h), xat(df, 0, s, -d, h), device(axis_of(s, 1), d)
        if kind == "m4":
            _, df, s, d = key
            return xat(df, 0, s, -d, fw(d)), xat(df, 0, s, 2, fw(d)), device(axis_of(s, 1), d)
        if kind == "m5":
            _, df, s, dg = key
            return xat(df, 0, s, dg), xat(df, 1, s, dg), other
        if kind == "r0":
            _, df, n = key
            part = pl.ds(n * (width // PIECES), width // PIECES)
            return ybuf.at[df, pl.ds(8 * ROWS, 8 * ROWS), part], sib.at[df, :, part], other
        if kind == "r1":
            _, df, s, d = key
            return yat(df, 0, s, 2, fw(d)), halves.at[df, s, fw(d)], device(axis_of(s, 1), d)
        if kind == "r2":
            _, df, s, d, h = key
            return yat(df, 0, s, d, h), fulls.at[df, s, fw(d), :, ycols(h)], device(axis_of(s, 1), d)
        if kind == "r3":
            _, s, d = key
            return yat(2, 0, s, 0, fw(d)), halves2.at[s, fw(d)], device(axis_of(s, 0), d)
        _, s, d, h = key
        return yat(d, 0, s, 0, h), fulls2.at[s, fw(d), :, ycols(h)], device(axis_of(s, 0), d)

    index = {key: i for i, key in enumerate(names)}

    def copy(key):
        src, dst, dev = ends(key)
        i = index[key]
        return pltpu.make_async_remote_copy(
            src_ref=src, dst_ref=dst, send_sem=ssem.at[i], recv_sem=rsem.at[i],
            device_id=dev, device_id_type=MESH)

    floats = tokens[...].astype(F32)
    meansq = jnp.mean(floats * floats, axis=1, keepdims=True)
    normed = (floats * lax.rsqrt(meansq + 1e-06) * gain[...]).astype(BF16)
    mixing = prob[...] / jnp.sum(prob[...], axis=1, keepdims=True)
    lane = lax.broadcasted_iota(jnp.int32, (2 * ROWS, EXTRA), 1)
    experts = local * SIDE * 2
    mix = jnp.zeros((2 * ROWS, EXTRA), F32)
    chosen = ids[...]
    for k in range(chosen.shape[1]):
        mine = jnp.broadcast_to(chosen[:, k:k + 1], lane.shape)
        mine = (mine == lane) | (mine + experts == lane)
        mix = mix + jnp.where(mine, jnp.broadcast_to(mixing[:, k:k + 1], lane.shape), 0.0)
    coarse = mix.astype(BF16)
    fine = (mix - coarse.astype(F32)).astype(BF16)
    packed = jnp.where(lane < experts, coarse.astype(F32), fine.astype(F32)).astype(BF16)
    for s in (0, 1):
        xbuf[0, rows(0, s, 0), pl.ds(0, width)] = normed[s * ROWS:(s + 1) * ROWS]
        xbuf[0, rows(0, s, 0), pl.ds(width, EXTRA)] = packed[s * ROWS:(s + 1) * ROWS]
    pl.semaphore_wait(barrier, len(partners))

    line = lax.broadcasted_iota(jnp.int32, (EXTRA, EXTRA), 0)

    def up(df, l):
        both = jnp.dot(xbuf[df, :, pl.ds(0, width)], w1[l], preferred_element_type=F32)
        e = exp * local + l
        pick = jnp.where((line == e) | (line == e + experts), 1.0, 0.0).astype(BF16)
        weight = jnp.dot(xbuf[df, :, pl.ds(width, EXTRA)], pick, preferred_element_type=F32)
        for c in range(0, hidden, EXTRA):
            g, u = both[:, c:c + EXTRA], both[:, hidden + c:hidden + c + EXTRA]
            hid[:, pl.ds(l * hidden + c, EXTRA)] = (g / (1.0 + jnp.exp(-g)) * u * weight).astype(BF16)

    def down(df, n):
        part = pl.ds(n * (width // PIECES), width // PIECES)
        ybuf[df, :, part] = jnp.dot(hid[...], w2[:, part], preferred_element_type=F32).astype(BF16)

    def total(df, s, dg, h):
        own = ybuf[df, rows(0, s, dg), ycols(h)].astype(F32)
        return own + sib[df, rows(0, s, dg), ycols(h)].astype(F32)

    got = set()
    loaded = set()

    def load_wait(which):
        for i in which:
            if i not in loaded:
                loaded.add(i)
                loads[i].wait()

    for key in order:
        needs, after, dur, sends, prio = tasks[key]
        for m in needs:
            if m not in got:
                got.add(m)
                copy(m).wait_recv()
        kind = key[0]
        if kind == "U":
            load_wait((2 * key[2], 2 * key[2] + 1))
            up(key[1], key[2])
        elif kind == "D":
            load_wait((4, 5))
            down(key[1], key[2])
        elif kind == "p2":
            _, df, h = key
            for s in (0, 1):
                ybuf[df, rows(0, s, 2), ycols(h)] = total(df, s, 2, h).astype(BF16)
            for s in (0, 1):
                ybuf[df, rows(0, s, -toward(h)), ycols(h)] = total(df, s, -toward(h), h).astype(BF16)
        elif kind == "p13":
            _, df, s, h = key
            t = toward(h)
            ybuf[df, rows(0, s, t), ycols(h)] = (total(df, s, t, h) + halves[df, s, h].astype(F32)).astype(BF16)
        elif kind == "p0":
            _, df, s, h = key
            whole = total(df, s, 0, h)
            for i in (0, 1):
                whole = whole + fulls[df, s, i, :, ycols(h)].astype(F32)
            if df == 0:
                for i in (0, 1):
                    whole = whole + fulls2[s, i, :, ycols(h)].astype(F32)
                out[pl.ds(s * ROWS, ROWS), ycols(h)] = whole.astype(BF16)
            else:
                if df != 2 and h == fw(1 if df == 1 else -1):
                    whole = whole + halves2[s, h].astype(F32)
                ybuf[df, rows(0, s, 0), ycols(h)] = whole.astype(BF16)
        for m in sends:
            copy(m).start()
    for m in names:
        copy(m).wait_send()


def per_device(tokens, norm_gain, expert_ids, gate_prob, w_gate, w_up, w_down):
    count, width = tokens.shape
    local, _, hidden = w_gate.shape
    order, tasks, names, _, _, _ = plan(width)
    vmem = pl.BlockSpec(memory_space=pltpu.VMEM)
    hbm = pl.BlockSpec(memory_space=pl.ANY)
    chunk = 2 * 2 * SIDE * ROWS
    return pl.pallas_call(
        functools.partial(kernel, order, tasks, names),
        out_shape=jax.ShapeDtypeStruct((count, width), BF16),
        in_specs=[vmem] * 4 + [hbm] * 3,
        out_specs=vmem,
        scratch_shapes=[
            pltpu.VMEM((SIDE, chunk, width + EXTRA), BF16),
            pltpu.VMEM((local, width, 2 * hidden), BF16),
            pltpu.VMEM((local * hidden, width), BF16),
            pltpu.VMEM((chunk, local * hidden), BF16),
            pltpu.VMEM((SIDE, chunk, width), BF16),
            pltpu.VMEM((SIDE, chunk // 2, width), BF16),
            pltpu.VMEM((SIDE, 2, 2, ROWS, width // 2), BF16),
            pltpu.VMEM((SIDE, 2, 2, ROWS, width), BF16),
            pltpu.VMEM((2, 2, ROWS, width // 2), BF16),
            pltpu.VMEM((2, 2, ROWS, width), BF16),
            pltpu.SemaphoreType.DMA((3 * local,)),
            pltpu.SemaphoreType.DMA((len(names),)),
            pltpu.SemaphoreType.DMA((len(names),)),
        ],
        compiler_params=pltpu.CompilerParams(
            collective_id=0, has_side_effects=True, vmem_limit_bytes=60 * 1024 * 1024),
        name="experts",
    )(tokens, norm_gain.reshape(1, width), expert_ids, gate_prob, w_gate, w_up, w_down)


def solution(mesh):
    placed = (
        P(("grp", "exp", "ten"), None),
        P(),
        P(("grp", "exp", "ten"), None),
        P(("grp", "exp", "ten"), None),
        P("exp", None, "ten"),
        P("exp", None, "ten"),
        P("exp", "ten", None),
    )
    return jax.shard_map(
        per_device,
        mesh=mesh,
        in_specs=placed,
        out_specs=P(("grp", "exp", "ten"), None),
        check_vma=False,
    )
```

```python
import functools

import jax
import jax.numpy as jnp
from jax import lax
from jax.experimental import pallas as pl
from jax.experimental.pallas import tpu as pltpu
from jax.sharding import PartitionSpec as P

MESH = pl.DeviceIdType.MESH
BF16, F32 = jnp.bfloat16, jnp.float32
SIDE = 4
ROWS = 16
EXTRA = 128
PIECES = 4
DIRS = (1, -1)
ORDER = (
    ("m3", 0, 1, 1, 0), ("m1", 0, 1, 0), ("m1", 0, 1, 1), ("m1", 1, 1, 1), ("m3", 0, 1, -1, 1), ("m3", 0, 0, 1, 0),
    ("m1", 1, 1, 0), ("m5", 0, 0, 0), ("m3", 0, 1, 1, 1), ("m3", 0, 0, -1, 1), ("m5", 0, 1, 0), ("m3", 0, 1, -1, 0),
    ("m1", 1, -1, 1), ("m1", 0, -1, 1), ("m3", 0, 0, -1, 0), ("m3", 0, 0, 1, 1), ("m4", 0, 0, -1), ("m5", 0, 1, 1),
    ("m4", 0, 1, -1), ("m4", 0, 1, 1), ("m3", 3, 0, -1, 1), ("m4", 0, 0, 1), ("m3", 3, 0, -1, 0), ("m3", 3, 1, 1, 0),
    ("m3", 3, 1, -1, 1), ("m3", 3, 1, -1, 0), ("m2", 1, -1), ("m2", 0, -1), ("m3", 3, 0, 1, 0), ("m5", 0, 0, 1),
    ("m1", 0, -1, 0), ("m2", 1, 1), ("m5", 3, 0, 0), ("m3", 3, 0, 1, 1), ("m2", 0, 1), ("m5", 0, 0, 3),
    ("m5", 0, 1, 3), ("m5", 0, 1, 2), ("m4", 3, 0, -1), ("m1", 1, -1, 0), ("m3", 3, 1, 1, 1), ("m5", 0, 0, 2),
    ("m4", 3, 1, 1), ("m4", 3, 0, 1), ("m4", 3, 1, -1), ("m5", 3, 0, 1), ("U", 0, 0), ("m5", 2, 0, 0),
    ("m3", 2, 0, -1, 1), ("m3", 2, 1, -1, 1), ("m3", 1, 1, -1, 1), ("m5", 2, 1, 0), ("m5", 3, 1, 1),
    ("m3", 2, 1, -1, 0), ("m3", 2, 0, 1, 0), ("m3", 2, 0, 1, 1), ("m5", 3, 1, 0), ("m3", 2, 1, 1, 1),
    ("m3", 2, 0, -1, 0), ("m3", 1, 0, -1, 1), ("m3", 2, 1, 1, 0), ("m5", 3, 1, 3), ("U", 0, 1), ("m5", 3, 0, 2),
    ("m3", 1, 1, 1, 1), ("m5", 3, 0, 3), ("m5", 3, 1, 2), ("D", 0, 0), ("D", 0, 3), ("r0", 0, 0), ("m3", 1, 1, 1, 0),
    ("r0", 0, 3), ("D", 0, 1), ("r0", 0, 1), ("m4", 2, 0, 1), ("D", 0, 2), ("r0", 0, 2), ("m5", 1, 0, 0),
    ("m3", 1, 0, 1, 1), ("m3", 1, 0, 1, 0), ("m4", 2, 1, -1), ("m4", 2, 0, -1), ("m4", 2, 1, 1), ("U", 3, 1),
    ("m5", 2, 0, 1), ("m5", 2, 1, 3), ("U", 3, 0), ("m5", 2, 0, 3), ("q", 0, 1, 2, 0), ("r1", 0, 1, 1),
    ("m5", 1, 1, 0), ("m3", 1, 1, -1, 0), ("D", 3, 3), ("q", 0, 1, -1, 0), ("m5", 2, 0, 2), ("m4", 1, 0, -1),
    ("q", 0, 1, 2, 1), ("m5", 2, 1, 2), ("m5", 2, 1, 1), ("m3", 1, 0, -1, 0), ("q", 0, 0, -1, 0), ("q", 0, 0, 2, 1),
    ("D", 3, 2), ("q", 0, 1, 1, 1), ("r0", 3, 2), ("r1", 0, 1, -1), ("D", 3, 1), ("r0", 3, 1), ("m4", 1, 1, 1),
    ("m4", 1, 0, 1), ("q", 0, 0, 1, 1), ("D", 3, 0), ("r0", 3, 3), ("q", 0, 1, 1, 0), ("r2", 0, 1, 1, 1),
    ("r2", 0, 1, -1, 0), ("r2", 0, 1, 1, 0), ("m5", 1, 1, 1), ("q", 0, 0, 2, 0), ("r1", 0, 0, 1), ("m4", 1, 1, -1),
    ("U", 2, 0), ("r0", 3, 0), ("U", 2, 1), ("m5", 1, 0, 3), ("q", 3, 0, 2, 1), ("r1", 3, 0, -1), ("m5", 1, 0, 1),
    ("q", 0, 1, -1, 1), ("q", 3, 1, 1, 1), ("m5", 1, 1, 3), ("D", 2, 1), ("m5", 1, 0, 2), ("q", 3, 1, 2, 0),
    ("r2", 0, 0, 1, 1), ("q", 3, 0, -1, 0), ("r2", 3, 0, -1, 0), ("r2", 0, 1, -1, 1), ("r2", 0, 0, -1, 0),
    ("q", 3, 0, 1, 1), ("m5", 1, 1, 2), ("q", 3, 0, 2, 0), ("r1", 3, 0, 1), ("r1", 3, 1, 1), ("r0", 2, 1),
    ("q", 3, 1, -1, 0), ("D", 2, 2), ("r2", 3, 1, -1, 0), ("D", 2, 0), ("r2", 3, 1, 1, 1), ("r2", 3, 0, 1, 1),
    ("r0", 2, 0), ("D", 2, 3), ("r0", 2, 3), ("r1", 0, 0, -1), ("r0", 2, 2), ("U", 1, 1), ("q", 2, 1, 2, 0),
    ("r1", 2, 1, 1), ("q", 2, 1, -1, 0), ("r2", 2, 1, -1, 0), ("q", 2, 0, 2, 0), ("r1", 2, 0, 1), ("q", 3, 0, 1, 0),
    ("r2", 3, 0, 1, 0), ("q", 3, 0, -1, 1), ("r2", 3, 0, -1, 1), ("q", 3, 1, 2, 1), ("r1", 3, 1, -1), ("U", 1, 0),
    ("D", 1, 3), ("r0", 1, 3), ("q", 2, 0, 2, 1), ("r1", 2, 0, -1), ("q", 2, 1, 2, 1), ("r1", 2, 1, -1), ("D", 1, 2),
    ("r0", 1, 2), ("q", 2, 0, 1, 1), ("r2", 2, 0, 1, 1), ("q", 3, 1, 1, 0), ("r2", 3, 1, 1, 0), ("q", 2, 0, -1, 0),
    ("r2", 2, 0, -1, 0), ("D", 1, 1), ("q", 2, 1, 1, 0), ("r0", 1, 1), ("q", 3, 1, -1, 1), ("r2", 3, 1, -1, 1),
    ("q", 2, 0, 1, 0), ("r2", 2, 1, 1, 0), ("r2", 2, 0, 1, 0), ("D", 1, 0), ("r0", 1, 0), ("q", 1, 0, 2, 1),
    ("r1", 1, 0, -1), ("q", 2, 0, -1, 1), ("r2", 2, 0, -1, 1), ("q", 1, 1, 2, 1), ("r1", 1, 1, -1),
    ("q", 1, 0, 1, 1), ("r2", 1, 0, 1, 1), ("q", 2, 1, 1, 1), ("q", 2, 1, -1, 1), ("r2", 2, 1, 1, 1),
    ("r2", 2, 1, -1, 1), ("q", 1, 0, -1, 0), ("r2", 1, 0, -1, 0), ("q", 1, 1, 2, 0), ("r1", 1, 1, 1),
    ("q", 1, 0, 2, 0), ("r1", 1, 0, 1), ("q", 2, 0, 0, 0), ("q", 2, 1, 0, 0), ("q", 1, 0, -1, 1), ("r3", 1, 1),
    ("r2", 1, 0, -1, 1), ("q", 0, 0, -1, 1), ("q", 1, 1, -1, 1), ("r2", 1, 1, -1, 1), ("r3", 0, 1),
    ("q", 1, 1, -1, 0), ("q", 2, 0, 0, 1), ("r3", 0, -1), ("q", 1, 1, 1, 1), ("r2", 1, 1, 1, 1), ("q", 2, 1, 0, 1),
    ("r3", 1, -1), ("r2", 1, 1, -1, 0), ("r2", 0, 0, -1, 1), ("q", 1, 1, 1, 0), ("q", 1, 0, 1, 0),
    ("r2", 1, 0, 1, 0), ("q", 0, 0, 1, 0), ("r2", 0, 0, 1, 0), ("q", 3, 1, 0, 0), ("q", 3, 0, 0, 0),
    ("r2", 1, 1, 1, 0), ("r4", 0, -1, 0), ("r4", 1, -1, 0), ("q", 1, 0, 0, 1), ("r4", 0, 1, 1), ("q", 1, 1, 0, 1),
    ("r4", 1, 1, 1), ("q", 3, 1, 0, 1), ("q", 3, 0, 0, 1), ("r4", 1, -1, 1), ("q", 1, 0, 0, 0), ("r4", 0, -1, 1),
    ("r4", 0, 1, 0), ("q", 1, 1, 0, 0), ("r4", 1, 1, 0), ("q", 0, 0, 0, 1), ("q", 0, 0, 0, 0), ("q", 0, 1, 0, 1),
    ("q", 0, 1, 0, 0),
)
SENT = tuple(k for k in ORDER if k[0] not in ("U", "D", "q"))


def fw(d):
    return 0 if d == 1 else 1


def toward(h):
    return 1 if h == 0 else -1


def axis_of(s, second):
    return (s + second) % 2


def gathered(df, s, dg):
    if dg == 2:
        return [("m4", df, s, d) for d in DIRS]
    if dg:
        return [("m3", df, s, 1 if dg == 3 else -1, h) for h in (0, 1)]
    if df == 2:
        return [("m2", s, d) for d in DIRS]
    return [("m1", s, 1 if df == 3 else -1, h) for h in (0, 1)] if df else []


def needs(key):
    kind = key[0]
    if kind == "m2":
        return [("m1", key[1], key[2], fw(key[2]))]
    if kind == "m3":
        _, df, s, d, h = key
        return [m for m in gathered(df, s, 0) if (fw(m[2]) if m[0] == "m2" else m[3]) == h]
    if kind == "m4":
        return [("m3", key[1], key[2], key[3], fw(key[3]))]
    if kind == "m5":
        return gathered(*key[1:])
    if kind == "U":
        found = []
        for s in (0, 1):
            for dg in range(SIDE):
                found += gathered(key[1], s, dg) + [("m5", key[1], s, dg)]
        return found
    if kind == "q":
        _, df, s, dg, h = key
        t = toward(h)
        found = [("r0", df, n) for n in range(h * PIECES // 2, (h + 1) * PIECES // 2)]
        if dg == t:
            found.append(("r1", df, s, t))
        if dg == 0:
            found += [("r2", df, s, d, h) for d in DIRS]
            if df == 0:
                found += [("r4", s, d, h) for d in DIRS]
            elif df == t % SIDE:
                found.append(("r3", s, t))
        return found
    return []


def kernel(tokens_hbm, gain_hbm, ids_hbm, prob_hbm, wg, wu, wd, out, tokens, gain, ids, prob,
           xbuf, w1, w2, hid, ybuf, sib, halves, fulls, halves2, fulls2, isem, wsem, ssem, rsem):
    exp, ten = lax.axis_index("exp"), lax.axis_index("ten")
    cx, core = exp // 2, exp % 2
    width = tokens.shape[1]
    half = width // 2
    hidden = wg.shape[2]
    local = wg.shape[0]
    xcut = (width + EXTRA) // 256 * 128 + 128

    def device(axis, d):
        if axis == 0:
            return {"exp": (cx + SIDE + d) % SIDE * 2 + core, "ten": ten}
        return {"exp": exp, "ten": (ten + SIDE + d) % SIDE}

    other = {"exp": cx * 2 + 1 - core, "ten": ten}
    partners = [device(a, d) for a in (0, 1) for d in DIRS] + [other]
    barrier = pltpu.get_barrier_semaphore()
    for p in partners:
        pl.semaphore_signal(barrier, inc=1, device_id=p, device_id_type=MESH)

    small = [pltpu.make_async_copy(a, b, isem.at[i]) for i, (a, b) in enumerate(
        ((tokens_hbm, tokens), (ids_hbm, ids), (prob_hbm, prob), (gain_hbm, gain)))]
    loads = []
    for l in range(local):
        loads.append(pltpu.make_async_copy(wg.at[l], w1.at[l, :, pl.ds(0, hidden)], wsem.at[3 * l]))
        loads.append(pltpu.make_async_copy(wu.at[l], w1.at[l, :, pl.ds(hidden, hidden)], wsem.at[3 * l + 1]))
    for l in range(local):
        loads.append(pltpu.make_async_copy(wd.at[l], w2.at[pl.ds(l * hidden, hidden)], wsem.at[3 * l + 2]))
    for c in small + loads:
        c.start()

    def rows(k, s, dg):
        return pl.ds(((k * 2 + s) * SIDE + dg % SIDE) * ROWS, ROWS)

    def xcols(h):
        return pl.ds(0, xcut) if h == 0 else pl.ds(xcut, width + EXTRA - xcut)

    def ycols(h):
        return pl.ds(h * half, half)

    def xat(df, k, s, dg, h=None):
        if h is None:
            return xbuf.at[df % SIDE, rows(k, s, dg)]
        return xbuf.at[df % SIDE, rows(k, s, dg), xcols(h)]

    def yat(df, k, s, dg, h):
        return ybuf.at[df % SIDE, rows(k, s, dg), ycols(h)]

    def ends(key):
        kind = key[0]
        if kind == "m1":
            _, s, d, h = key
            return xat(0, 0, s, 0, h), xat(-d, 0, s, 0, h), device(axis_of(s, 0), d)
        if kind == "m2":
            _, s, d = key
            return xat(-d, 0, s, 0, fw(d)), xat(2, 0, s, 0, fw(d)), device(axis_of(s, 0), d)
        if kind == "m3":
            _, df, s, d, h = key
            return xat(df, 0, s, 0, h), xat(df, 0, s, -d, h), device(axis_of(s, 1), d)
        if kind == "m4":
            _, df, s, d = key
            return xat(df, 0, s, -d, fw(d)), xat(df, 0, s, 2, fw(d)), device(axis_of(s, 1), d)
        if kind == "m5":
            _, df, s, dg = key
            return xat(df, 0, s, dg), xat(df, 1, s, dg), other
        if kind == "r0":
            _, df, n = key
            part = pl.ds(n * (width // PIECES), width // PIECES)
            return ybuf.at[df, pl.ds(8 * ROWS, 8 * ROWS), part], sib.at[df, :, part], other
        if kind == "r1":
            _, df, s, d = key
            return yat(df, 0, s, 2, fw(d)), halves.at[df, s, fw(d)], device(axis_of(s, 1), d)
        if kind == "r2":
            _, df, s, d, h = key
            return yat(df, 0, s, d, h), fulls.at[df, s, fw(d), :, ycols(h)], device(axis_of(s, 1), d)
        if kind == "r3":
            _, s, d = key
            return yat(2, 0, s, 0, fw(d)), halves2.at[s, fw(d)], device(axis_of(s, 0), d)
        _, s, d, h = key
        return yat(d, 0, s, 0, h), fulls2.at[s, fw(d), :, ycols(h)], device(axis_of(s, 0), d)

    index = {key: i for i, key in enumerate(SENT)}

    def copy(key):
        src, dst, dev = ends(key)
        i = index[key]
        return pltpu.make_async_remote_copy(
            src_ref=src, dst_ref=dst, send_sem=ssem.at[i], recv_sem=rsem.at[i],
            device_id=dev, device_id_type=MESH)

    step = 4 * EXTRA
    count = tokens.shape[0]
    small[0].wait()
    squares = jnp.zeros((count, EXTRA), F32)
    for c in range(0, width, EXTRA):
        piece = tokens[:, c:c + EXTRA].astype(F32)
        squares = squares + piece * piece
    scale = lax.rsqrt(jnp.sum(squares, axis=1, keepdims=True) / width + 1e-06)
    small[3].wait()
    for s in (0, 1):
        scale_s = jnp.broadcast_to(scale[s * ROWS:(s + 1) * ROWS], (ROWS, step))
        for c in range(0, width, step):
            piece = tokens[s * ROWS:(s + 1) * ROWS, c:c + step].astype(F32)
            xbuf[0, rows(0, s, 0), pl.ds(c, step)] = (piece * scale_s * gain[:, c:c + step]).astype(BF16)
    small[1].wait()
    small[2].wait()
    experts = local * SIDE * 2
    mixing = prob[...] / jnp.sum(prob[...], axis=0, keepdims=True)
    chosen = ids[...]
    line = lax.broadcasted_iota(jnp.int32, (2 * experts, count), 0)
    number = jnp.where(line >= experts, line - experts, line)
    mix = jnp.zeros((2 * experts, count), F32)
    for k in range(chosen.shape[0]):
        mine = jnp.broadcast_to(chosen[k:k + 1], line.shape) == number
        mix = mix + jnp.where(mine, jnp.broadcast_to(mixing[k:k + 1], line.shape), 0.0)
    coarse = mix.astype(BF16).astype(F32)
    terms = jnp.where(line >= experts, mix - coarse, coarse).astype(BF16)
    eye = (lax.broadcasted_iota(jnp.int32, (2 * experts, EXTRA), 0)
           == lax.broadcasted_iota(jnp.int32, (2 * experts, EXTRA), 1))
    packed = lax.dot_general(terms, jnp.where(eye, 1.0, 0.0).astype(BF16), (((0,), (0,)), ((), ())),
                             preferred_element_type=F32).astype(BF16)
    for s in (0, 1):
        xbuf[0, rows(0, s, 0), pl.ds(width, EXTRA)] = packed[s * ROWS:(s + 1) * ROWS]
    pl.semaphore_wait(barrier, len(partners))

    lane_line = lax.broadcasted_iota(jnp.int32, (EXTRA, EXTRA), 0)

    def up(df, l):
        both = jnp.dot(xbuf[df, :, pl.ds(0, width)], w1[l], preferred_element_type=F32)
        e = exp * local + l
        pick = jnp.where((lane_line == e) | (lane_line == e + experts), 1.0, 0.0).astype(BF16)
        weight = jnp.dot(xbuf[df, :, pl.ds(width, EXTRA)], pick, preferred_element_type=F32)
        for c in range(0, hidden, EXTRA):
            g, u = both[:, c:c + EXTRA], both[:, hidden + c:hidden + c + EXTRA]
            hid[df, :, pl.ds(l * hidden + c, EXTRA)] = (g / (1.0 + jnp.exp(-g)) * u * weight).astype(BF16)

    def down(df, n):
        part = pl.ds(n * (width // PIECES), width // PIECES)
        ybuf[df, :, part] = jnp.dot(hid[df], w2[:, part], preferred_element_type=F32).astype(BF16)

    def add(df, s, dg, h):
        t = toward(h)
        whole = ybuf[df, rows(0, s, dg), ycols(h)].astype(F32) + sib[df, rows(0, s, dg), ycols(h)].astype(F32)
        if dg == t:
            whole = whole + halves[df, s, h].astype(F32)
        if dg == 0:
            for i in (0, 1):
                whole = whole + fulls[df, s, i, :, ycols(h)].astype(F32)
            if df == 0:
                for i in (0, 1):
                    whole = whole + fulls2[s, i, :, ycols(h)].astype(F32)
                out[pl.ds(s * ROWS, ROWS), ycols(h)] = whole.astype(BF16)
                return
            if df == t % SIDE:
                whole = whole + halves2[s, h].astype(F32)
        ybuf[df, rows(0, s, dg), ycols(h)] = whole.astype(BF16)

    got, loaded = set(), set()

    def load_wait(which):
        for i in which:
            if i not in loaded:
                loaded.add(i)
                loads[i].wait()

    for key in ORDER:
        for m in needs(key):
            if m not in got:
                got.add(m)
                copy(m).wait_recv()
        if key[0] == "U":
            load_wait((2 * key[2], 2 * key[2] + 1))
            up(key[1], key[2])
        elif key[0] == "D":
            load_wait((4, 5))
            down(key[1], key[2])
        elif key[0] == "q":
            add(*key[1:])
        else:
            copy(key).start()
    for m in SENT:
        copy(m).wait_send()


def per_device(tokens, norm_gain, expert_ids, gate_prob, w_gate, w_up, w_down):
    count, width = tokens.shape
    top = expert_ids.shape[1]
    local, _, hidden = w_gate.shape
    hbm = pl.BlockSpec(memory_space=pl.ANY)
    chunk = 2 * 2 * SIDE * ROWS
    return pl.pallas_call(
        kernel,
        out_shape=jax.ShapeDtypeStruct((count, width), BF16),
        in_specs=[hbm] * 7,
        out_specs=pl.BlockSpec(memory_space=pltpu.VMEM),
        scratch_shapes=[
            pltpu.VMEM((count, width), BF16),
            pltpu.VMEM((1, width), F32),
            pltpu.VMEM((top, count), jnp.int32),
            pltpu.VMEM((top, count), F32),
            pltpu.VMEM((SIDE, chunk, width + EXTRA), BF16),
            pltpu.VMEM((local, width, 2 * hidden), BF16),
            pltpu.VMEM((local * hidden, width), BF16),
            pltpu.VMEM((SIDE, chunk, local * hidden), BF16),
            pltpu.VMEM((SIDE, chunk, width), BF16),
            pltpu.VMEM((SIDE, chunk // 2, width), BF16),
            pltpu.VMEM((SIDE, 2, 2, ROWS, width // 2), BF16),
            pltpu.VMEM((SIDE, 2, 2, ROWS, width), BF16),
            pltpu.VMEM((2, 2, ROWS, width // 2), BF16),
            pltpu.VMEM((2, 2, ROWS, width), BF16),
            pltpu.SemaphoreType.DMA((4,)),
            pltpu.SemaphoreType.DMA((3 * local,)),
            pltpu.SemaphoreType.DMA((len(SENT),)),
            pltpu.SemaphoreType.DMA((len(SENT),)),
        ],
        compiler_params=pltpu.CompilerParams(
            collective_id=0, has_side_effects=True, vmem_limit_bytes=60 * 1024 * 1024),
        name="experts",
    )(tokens, norm_gain.reshape(1, width), expert_ids.T, gate_prob.T, w_gate, w_up, w_down)


def solution(mesh):
    placed = (
        P(("grp", "exp", "ten"), None),
        P(),
        P(("grp", "exp", "ten"), None),
        P(("grp", "exp", "ten"), None),
        P("exp", None, "ten"),
        P("exp", None, "ten"),
        P("exp", "ten", None),
    )
    return jax.shard_map(
        per_device,
        mesh=mesh,
        in_specs=placed,
        out_specs=P(("grp", "exp", "ten"), None),
        check_vma=False,
    )
```

```python
import functools

import jax
import jax.numpy as jnp
from jax import lax
from jax.experimental import pallas as pl
from jax.experimental.pallas import tpu as pltpu
from jax.sharding import PartitionSpec as P

MESH = pl.DeviceIdType.MESH
BF16, F32 = jnp.bfloat16, jnp.float32
SIDE = 4
ROWS = 16
EXTRA = 128
PIECES = 4
DIRS = (1, -1)
ORDER = (
    ("m1", 0, -1, 0), ("m3", 0, 1, 1, 0), ("m3", 0, 0, 1, 0), ("m3", 0, 0, -1, 1), ("m1", 1, -1, 1), ("m1", 0, 1, 0),
    ("m1", 1, 1, 0), ("m1", 1, -1, 0), ("m5", 0, 0, 0), ("m3", 0, 1, -1, 1), ("m1", 0, -1, 1), ("m3", 0, 1, 1, 1),
    ("m3", 0, 1, -1, 0), ("m3", 0, 0, 1, 1), ("m4", 0, 1, 1), ("m4", 0, 0, 1), ("m4", 0, 0, -1), ("m3", 1, 0, 1, 0),
    ("m1", 0, 1, 1), ("m3", 0, 0, -1, 0), ("m4", 0, 1, -1), ("m3", 1, 1, -1, 1), ("m3", 1, 1, 1, 0), ("m5", 1, 1, 0),
    ("m5", 0, 1, 0), ("m3", 1, 0, -1, 1), ("m5", 1, 0, 0), ("m2", 1, 1), ("m2", 0, -1), ("m2", 0, 1),
    ("m5", 0, 0, 3), ("m3", 1, 1, -1, 0), ("m3", 1, 1, 1, 1), ("m2", 1, -1), ("m3", 1, 0, 1, 1), ("m5", 0, 1, 3),
    ("m1", 1, 1, 1), ("m5", 0, 1, 1), ("m5", 0, 0, 2), ("m5", 0, 1, 2), ("m5", 0, 0, 1), ("m3", 1, 0, -1, 0),
    ("m4", 1, 0, -1), ("m5", 3, 0, 0), ("m4", 1, 1, 1), ("m3", 2, 1, 1, 0), ("m4", 1, 0, 1), ("m3", 3, 1, 1, 0),
    ("m4", 1, 1, -1), ("m3", 3, 0, 1, 0), ("m3", 2, 1, -1, 0), ("U", 0, 1), ("m3", 2, 1, -1, 1), ("m5", 2, 0, 0),
    ("m5", 1, 0, 3), ("m3", 2, 0, 1, 0), ("m3", 2, 0, -1, 1), ("m5", 2, 1, 0), ("m5", 1, 1, 3), ("m5", 1, 1, 1),
    ("m3", 2, 0, -1, 0), ("m3", 3, 0, -1, 1), ("m5", 1, 0, 1), ("U", 0, 0), ("m3", 2, 0, 1, 1), ("m5", 1, 0, 2),
    ("m5", 1, 1, 2), ("D", 0, 1), ("m3", 3, 1, -1, 1), ("m5", 3, 1, 0), ("m3", 3, 1, -1, 0), ("m3", 3, 1, 1, 1),
    ("D", 0, 2), ("r0", 0, 1), ("r0", 0, 2), ("D", 0, 3), ("r0", 0, 3), ("D", 0, 0), ("m4", 2, 0, -1),
    ("m4", 2, 1, -1), ("m3", 2, 1, 1, 1), ("m5", 2, 1, 1), ("m4", 2, 1, 1), ("m3", 3, 0, -1, 0), ("r0", 0, 0),
    ("m4", 2, 0, 1), ("U", 1, 0), ("m5", 2, 0, 3), ("m5", 2, 0, 1), ("q", 0, 1, 1, 1), ("r2", 0, 1, 1, 1),
    ("m4", 3, 0, -1), ("m4", 3, 0, 1), ("U", 1, 1), ("q", 0, 0, 1, 1), ("q", 0, 1, 2, 0), ("q", 0, 1, -1, 0),
    ("r2", 0, 1, -1, 0), ("r2", 0, 0, 1, 1), ("m5", 2, 1, 3), ("q", 0, 0, 2, 0), ("m5", 2, 0, 2), ("m3", 3, 0, 1, 1),
    ("m5", 3, 1, 3), ("q", 0, 0, 2, 1), ("r1", 0, 0, -1), ("D", 1, 0), ("m5", 2, 1, 2), ("r1", 0, 0, 1), ("D", 1, 2),
    ("D", 1, 1), ("m4", 3, 1, 1), ("r0", 1, 1), ("r0", 1, 0), ("r0", 1, 2), ("m4", 3, 1, -1), ("D", 1, 3),
    ("r0", 1, 3), ("m5", 3, 1, 1), ("m5", 3, 0, 1), ("m5", 3, 0, 2), ("U", 2, 1), ("U", 2, 0), ("m5", 3, 0, 3),
    ("m5", 3, 1, 2), ("q", 1, 1, 2, 1), ("D", 2, 3), ("r0", 2, 3), ("r1", 1, 1, -1), ("q", 1, 0, -1, 0),
    ("r2", 1, 0, -1, 0), ("D", 2, 1), ("r0", 2, 1), ("D", 2, 2), ("r0", 2, 2), ("D", 2, 0), ("r0", 2, 0),
    ("q", 1, 0, 2, 1), ("q", 1, 1, -1, 0), ("r1", 0, 1, 1), ("r1", 1, 0, -1), ("q", 1, 0, 2, 0), ("U", 3, 1),
    ("q", 2, 0, 2, 0), ("r1", 2, 0, 1), ("r2", 1, 1, -1, 0), ("r1", 1, 0, 1), ("q", 1, 1, 2, 0), ("r1", 1, 1, 1),
    ("q", 2, 0, -1, 0), ("r2", 2, 0, -1, 0), ("q", 2, 1, 2, 0), ("r1", 2, 1, 1), ("q", 2, 0, 2, 1),
    ("q", 2, 0, 1, 1), ("r2", 2, 0, 1, 1), ("q", 2, 1, 2, 1), ("r1", 2, 0, -1), ("r1", 2, 1, -1), ("q", 2, 1, -1, 0),
    ("r2", 2, 1, -1, 0), ("q", 0, 1, 2, 1), ("q", 2, 1, 1, 1), ("U", 3, 0), ("r2", 2, 1, 1, 1), ("D", 3, 1),
    ("r0", 3, 1), ("q", 1, 0, -1, 1), ("r1", 0, 1, -1), ("r2", 1, 0, -1, 1), ("D", 3, 0), ("r0", 3, 0),
    ("q", 2, 0, 1, 0), ("r2", 2, 0, 1, 0), ("q", 1, 1, 1, 1), ("r2", 1, 1, 1, 1), ("D", 3, 3), ("r0", 3, 3),
    ("q", 2, 1, 1, 0), ("r2", 2, 1, 1, 0), ("q", 1, 0, 1, 1), ("r2", 1, 0, 1, 1), ("q", 2, 1, -1, 1),
    ("r2", 2, 1, -1, 1), ("q", 2, 0, -1, 1), ("r2", 2, 0, -1, 1), ("D", 3, 2), ("r0", 3, 2), ("q", 3, 0, 2, 0),
    ("r1", 3, 0, 1), ("q", 0, 0, -1, 0), ("r2", 0, 0, -1, 0), ("q", 3, 1, 2, 0), ("r1", 3, 1, 1), ("q", 1, 1, -1, 1),
    ("q", 0, 0, 1, 0), ("r2", 1, 1, -1, 1), ("q", 2, 0, 0, 0), ("r3", 0, 1), ("q", 1, 0, 1, 0), ("r2", 1, 0, 1, 0),
    ("q", 3, 0, 2, 1), ("r1", 3, 0, -1), ("q", 3, 1, 2, 1), ("r1", 3, 1, -1), ("q", 3, 0, 1, 1), ("r2", 3, 0, 1, 1),
    ("q", 3, 0, -1, 0), ("q", 3, 1, 1, 1), ("q", 3, 1, -1, 0), ("r2", 3, 1, -1, 0), ("r2", 3, 1, 1, 1),
    ("q", 2, 1, 0, 1), ("r2", 3, 0, -1, 0), ("q", 0, 1, 1, 0), ("q", 2, 0, 0, 1), ("r3", 0, -1), ("q", 3, 1, 1, 0),
    ("r2", 3, 1, 1, 0), ("r3", 1, -1), ("q", 3, 0, 1, 0), ("r2", 3, 0, 1, 0), ("q", 2, 1, 0, 0), ("r3", 1, 1),
    ("r2", 0, 0, 1, 0), ("q", 1, 1, 1, 0), ("r2", 1, 1, 1, 0), ("q", 3, 0, -1, 1), ("r2", 3, 0, -1, 1),
    ("q", 3, 1, -1, 1), ("r2", 3, 1, -1, 1), ("q", 1, 0, 0, 1), ("r4", 0, 1, 1), ("q", 0, 1, -1, 1),
    ("r2", 0, 1, -1, 1), ("q", 0, 0, -1, 1), ("r2", 0, 0, -1, 1), ("q", 1, 0, 0, 0), ("q", 3, 1, 0, 0),
    ("q", 3, 0, 0, 0), ("r4", 0, -1, 0), ("q", 1, 1, 0, 1), ("r4", 1, -1, 0), ("r4", 1, 1, 1), ("r4", 0, 1, 0),
    ("r2", 0, 1, 1, 0), ("q", 3, 0, 0, 1), ("r4", 0, -1, 1), ("q", 3, 1, 0, 1), ("r4", 1, -1, 1), ("q", 1, 1, 0, 0),
    ("r4", 1, 1, 0), ("q", 0, 0, 0, 0), ("q", 0, 0, 0, 1), ("q", 0, 1, 0, 1), ("q", 0, 1, 0, 0),
)
SENT = tuple(k for k in ORDER if k[0] not in ("U", "D", "q"))


def fw(d):
    return 0 if d == 1 else 1


def toward(h):
    return 1 if h == 0 else -1


def axis_of(s, second):
    return (s + second) % 2


def gathered(df, s, dg):
    if dg == 2:
        return [("m4", df, s, d) for d in DIRS]
    if dg:
        return [("m3", df, s, 1 if dg == 3 else -1, h) for h in (0, 1)]
    if df == 2:
        return [("m2", s, d) for d in DIRS]
    return [("m1", s, 1 if df == 3 else -1, h) for h in (0, 1)] if df else []


def needs(key):
    kind = key[0]
    if kind == "m2":
        return [("m1", key[1], key[2], fw(key[2]))]
    if kind == "m3":
        _, df, s, d, h = key
        return [m for m in gathered(df, s, 0) if (fw(m[2]) if m[0] == "m2" else m[3]) == h]
    if kind == "m4":
        return [("m3", key[1], key[2], key[3], fw(key[3]))]
    if kind == "m5":
        return gathered(*key[1:])
    if kind == "U":
        found = []
        for s in (0, 1):
            for dg in range(SIDE):
                found += gathered(key[1], s, dg) + [("m5", key[1], s, dg)]
        return found
    if kind == "q":
        _, df, s, dg, h = key
        t = toward(h)
        found = [("r0", df, n) for n in range(h * PIECES // 2, (h + 1) * PIECES // 2)]
        if dg == t:
            found.append(("r1", df, s, t))
        if dg == 0:
            found += [("r2", df, s, d, h) for d in DIRS]
            if df == 0:
                found += [("r4", s, d, h) for d in DIRS]
            elif df == t % SIDE:
                found.append(("r3", s, t))
        return found
    return []


def kernel(tokens_hbm, gain_hbm, ids_hbm, prob_hbm, wg, wu, wd, out_hbm, tokens, gain, ids, prob, out,
           xbuf, w1, w2, hid, ybuf, sib, halves, fulls, halves2, fulls2, isem, osem, wsem, ssem, rsem):
    exp, ten = lax.axis_index("exp"), lax.axis_index("ten")
    cx, core = exp // 2, exp % 2
    width = tokens.shape[1]
    half = width // 2
    hidden = wg.shape[2]
    local = wg.shape[0]
    xcut = (width + EXTRA) // 256 * 128 + 128

    def device(axis, d):
        if axis == 0:
            return {"exp": (cx + SIDE + d) % SIDE * 2 + core, "ten": ten}
        return {"exp": exp, "ten": (ten + SIDE + d) % SIDE}

    other = {"exp": cx * 2 + 1 - core, "ten": ten}
    partners = [device(a, d) for a in (0, 1) for d in DIRS] + [other]
    barrier = pltpu.get_barrier_semaphore()
    for p in partners:
        pl.semaphore_signal(barrier, inc=1, device_id=p, device_id_type=MESH)

    small = [pltpu.make_async_copy(a, b, isem.at[i]) for i, (a, b) in enumerate(
        ((tokens_hbm, tokens), (ids_hbm, ids), (prob_hbm, prob), (gain_hbm, gain)))]
    loads = []
    for l in range(local):
        loads.append(pltpu.make_async_copy(wg.at[l], w1.at[l, :, pl.ds(0, hidden)], wsem.at[3 * l]))
        loads.append(pltpu.make_async_copy(wu.at[l], w1.at[l, :, pl.ds(hidden, hidden)], wsem.at[3 * l + 1]))
    for l in range(local):
        loads.append(pltpu.make_async_copy(wd.at[l], w2.at[pl.ds(l * hidden, hidden)], wsem.at[3 * l + 2]))
    for c in small:
        c.start()

    def rows(k, s, dg):
        return pl.ds(((k * 2 + s) * SIDE + dg % SIDE) * ROWS, ROWS)

    def xcols(h):
        return pl.ds(0, xcut) if h == 0 else pl.ds(xcut, width + EXTRA - xcut)

    def ycols(h):
        return pl.ds(h * half, half)

    def xat(df, k, s, dg, h=None):
        if h is None:
            return xbuf.at[df % SIDE, rows(k, s, dg)]
        return xbuf.at[df % SIDE, rows(k, s, dg), xcols(h)]

    def yat(df, k, s, dg, h):
        return ybuf.at[df % SIDE, rows(k, s, dg), ycols(h)]

    def ends(key):
        kind = key[0]
        if kind == "m1":
            _, s, d, h = key
            return xat(0, 0, s, 0, h), xat(-d, 0, s, 0, h), device(axis_of(s, 0), d)
        if kind == "m2":
            _, s, d = key
            return xat(-d, 0, s, 0, fw(d)), xat(2, 0, s, 0, fw(d)), device(axis_of(s, 0), d)
        if kind == "m3":
            _, df, s, d, h = key
            return xat(df, 0, s, 0, h), xat(df, 0, s, -d, h), device(axis_of(s, 1), d)
        if kind == "m4":
            _, df, s, d = key
            return xat(df, 0, s, -d, fw(d)), xat(df, 0, s, 2, fw(d)), device(axis_of(s, 1), d)
        if kind == "m5":
            _, df, s, dg = key
            return xat(df, 0, s, dg), xat(df, 1, s, dg), other
        if kind == "r0":
            _, df, n = key
            part = pl.ds(n * (width // PIECES), width // PIECES)
            return ybuf.at[df, pl.ds(8 * ROWS, 8 * ROWS), part], sib.at[df, :, part], other
        if kind == "r1":
            _, df, s, d = key
            return yat(df, 0, s, 2, fw(d)), halves.at[df, s, fw(d)], device(axis_of(s, 1), d)
        if kind == "r2":
            _, df, s, d, h = key
            return yat(df, 0, s, d, h), fulls.at[df, s, fw(d), :, ycols(h)], device(axis_of(s, 1), d)
        if kind == "r3":
            _, s, d = key
            return yat(2, 0, s, 0, fw(d)), halves2.at[s, fw(d)], device(axis_of(s, 0), d)
        _, s, d, h = key
        return yat(d, 0, s, 0, h), fulls2.at[s, fw(d), :, ycols(h)], device(axis_of(s, 0), d)

    index = {key: i for i, key in enumerate(SENT)}

    def copy(key):
        src, dst, dev = ends(key)
        i = index[key]
        return pltpu.make_async_remote_copy(
            src_ref=src, dst_ref=dst, send_sem=ssem.at[i], recv_sem=rsem.at[i],
            device_id=dev, device_id_type=MESH)

    count = tokens.shape[0]
    small[1].wait()
    small[2].wait()
    experts = local * SIDE * 2
    mixing = prob[...] / jnp.sum(prob[...], axis=0, keepdims=True)
    chosen = ids[...]
    line = lax.broadcasted_iota(jnp.int32, (2 * experts, count), 0)
    number = jnp.where(line >= experts, line - experts, line)
    mix = jnp.zeros((2 * experts, count), F32)
    for k in range(chosen.shape[0]):
        mine = jnp.broadcast_to(chosen[k:k + 1], line.shape) == number
        mix = mix + jnp.where(mine, jnp.broadcast_to(mixing[k:k + 1], line.shape), 0.0)
    coarse = mix.astype(BF16).astype(F32)
    terms = jnp.where(line >= experts, mix - coarse, coarse).astype(BF16)
    eye = (lax.broadcasted_iota(jnp.int32, (2 * experts, EXTRA), 0)
           == lax.broadcasted_iota(jnp.int32, (2 * experts, EXTRA), 1))
    packed = lax.dot_general(terms, jnp.where(eye, 1.0, 0.0).astype(BF16), (((0,), (0,)), ((), ())),
                             preferred_element_type=F32).astype(BF16)
    for s in (0, 1):
        xbuf[0, rows(0, s, 0), pl.ds(width, EXTRA)] = packed[s * ROWS:(s + 1) * ROWS]
    step = 4 * EXTRA
    small[0].wait()
    squares = jnp.zeros((count, EXTRA), F32)
    for c in range(0, width, EXTRA):
        piece = tokens[:, c:c + EXTRA].astype(F32)
        squares = squares + piece * piece
    scale = lax.rsqrt(jnp.sum(squares, axis=1, keepdims=True) / width + 1e-06)
    small[3].wait()
    for s in (0, 1):
        scale_s = jnp.broadcast_to(scale[s * ROWS:(s + 1) * ROWS], (ROWS, step))
        for c in range(0, width, step):
            piece = tokens[s * ROWS:(s + 1) * ROWS, c:c + step].astype(F32)
            xbuf[0, rows(0, s, 0), pl.ds(c, step)] = (piece * scale_s * gain[:, c:c + step]).astype(BF16)
    pl.semaphore_wait(barrier, len(partners))

    lane_line = lax.broadcasted_iota(jnp.int32, (EXTRA, EXTRA), 0)

    def up(df, l):
        both = jnp.dot(xbuf[df, :, pl.ds(0, width)], w1[l], preferred_element_type=F32)
        e = exp * local + l
        pick = jnp.where((lane_line == e) | (lane_line == e + experts), 1.0, 0.0).astype(BF16)
        weight = jnp.dot(xbuf[df, :, pl.ds(width, EXTRA)], pick, preferred_element_type=F32)
        for c in range(0, hidden, EXTRA):
            g, u = both[:, c:c + EXTRA], both[:, hidden + c:hidden + c + EXTRA]
            hid[df, :, pl.ds(l * hidden + c, EXTRA)] = (g / (1.0 + jnp.exp(-g)) * u * weight).astype(BF16)

    def down(df, n):
        part = pl.ds(n * (width // PIECES), width // PIECES)
        ybuf[df, :, part] = jnp.dot(hid[df], w2[:, part], preferred_element_type=F32).astype(BF16)

    def add(df, s, dg, h):
        t = toward(h)
        whole = ybuf[df, rows(0, s, dg), ycols(h)].astype(F32) + sib[df, rows(0, s, dg), ycols(h)].astype(F32)
        if dg == t:
            whole = whole + halves[df, s, h].astype(F32)
        if dg == 0:
            for i in (0, 1):
                whole = whole + fulls[df, s, i, :, ycols(h)].astype(F32)
            if df == 0:
                for i in (0, 1):
                    whole = whole + fulls2[s, i, :, ycols(h)].astype(F32)
                out[pl.ds(s * ROWS, ROWS), ycols(h)] = whole.astype(BF16)
                place = pl.ds(s * ROWS, ROWS), ycols(h)
                results.append(pltpu.make_async_copy(out.at[place], out_hbm.at[place], osem.at[2 * s + h]))
                results[-1].start()
                return
            if df == t % SIDE:
                whole = whole + halves2[s, h].astype(F32)
        ybuf[df, rows(0, s, dg), ycols(h)] = whole.astype(BF16)

    results = []
    got, loaded = set(), set()

    def load_wait(which):
        for i in which:
            if i not in loaded:
                loaded.add(i)
                loads[i].wait()

    for key in ORDER:
        if needs(key) and not got:
            for c in loads:
                c.start()
        for m in needs(key):
            if m not in got:
                got.add(m)
                copy(m).wait_recv()
        if key[0] == "U":
            load_wait((2 * key[2], 2 * key[2] + 1))
            up(key[1], key[2])
        elif key[0] == "D":
            load_wait((4, 5))
            down(key[1], key[2])
        elif key[0] == "q":
            add(*key[1:])
        else:
            copy(key).start()
    for m in SENT:
        copy(m).wait_send()
    for c in results:
        c.wait()


def per_device(tokens, norm_gain, expert_ids, gate_prob, w_gate, w_up, w_down):
    count, width = tokens.shape
    top = expert_ids.shape[1]
    local, _, hidden = w_gate.shape
    hbm = pl.BlockSpec(memory_space=pl.ANY)
    chunk = 2 * 2 * SIDE * ROWS
    return pl.pallas_call(
        kernel,
        out_shape=jax.ShapeDtypeStruct((count, width), BF16),
        in_specs=[hbm] * 7,
        out_specs=hbm,
        scratch_shapes=[
            pltpu.VMEM((count, width), BF16),
            pltpu.VMEM((1, width), F32),
            pltpu.VMEM((top, count), jnp.int32),
            pltpu.VMEM((top, count), F32),
            pltpu.VMEM((count, width), BF16),
            pltpu.VMEM((SIDE, chunk, width + EXTRA), BF16),
            pltpu.VMEM((local, width, 2 * hidden), BF16),
            pltpu.VMEM((local * hidden, width), BF16),
            pltpu.VMEM((SIDE, chunk, local * hidden), BF16),
            pltpu.VMEM((SIDE, chunk, width), BF16),
            pltpu.VMEM((SIDE, chunk // 2, width), BF16),
            pltpu.VMEM((SIDE, 2, 2, ROWS, width // 2), BF16),
            pltpu.VMEM((SIDE, 2, 2, ROWS, width), BF16),
            pltpu.VMEM((2, 2, ROWS, width // 2), BF16),
            pltpu.VMEM((2, 2, ROWS, width), BF16),
            pltpu.SemaphoreType.DMA((4,)),
            pltpu.SemaphoreType.DMA((4,)),
            pltpu.SemaphoreType.DMA((3 * local,)),
            pltpu.SemaphoreType.DMA((len(SENT),)),
            pltpu.SemaphoreType.DMA((len(SENT),)),
        ],
        compiler_params=pltpu.CompilerParams(
            collective_id=0, has_side_effects=True, vmem_limit_bytes=60 * 1024 * 1024),
        name="experts",
    )(tokens, norm_gain.reshape(1, width), expert_ids.T, gate_prob.T, w_gate, w_up, w_down)


def solution(mesh):
    placed = (
        P(("grp", "exp", "ten"), None),
        P(),
        P(("grp", "exp", "ten"), None),
        P(("grp", "exp", "ten"), None),
        P("exp", None, "ten"),
        P("exp", None, "ten"),
        P("exp", "ten", None),
    )
    return jax.shard_map(
        per_device,
        mesh=mesh,
        in_specs=placed,
        out_specs=P(("grp", "exp", "ten"), None),
        check_vma=False,
    )
```
